32 devices in a mesh: tm: 16 (over z, x, core), space: 2 (over y).
Axes of the slice: x: 2, y: 2, z: 4, core: 2. Of those that a mesh axis runs over, the one named last changes fastest.
Arguments:
- snapshots: bfloat16 [512, 5, 4096], P('tm', None, 'space'), may hold values from -210 to 210, as said below
- basis: bfloat16 [2, 33, 16, 5, 4096], P(None, None, None, None, ('space', 'tm')), may hold values from -6 to 6
- mass_table: float32 [8, 64, 64], replicated, may hold values from -0.03 to 3, as said below
- elem_kind: int32 [64], P(('space', 'tm')), may hold values from 0 to 7
- offsets: int32 [8], replicated, may hold values from 0 to 256, as said below
Outputs:
- coeffs: float32 [2, 33, 8, 16], replicated
- new_basis: bfloat16 [2, 33, 16, 5, 4096], P(None, None, None, None, ('space', 'tm'))
The draws below stay inside these ranges and needn't reach their ends.
Inputs may be any that keep to these rules, and one draw needn't show every extreme that they name: `snapshots`: rows of flow data. `mass_table`: each block is symmetric and positive definite. `offsets`: some block starts at 0 and some at 256.
All inputs are finite; a program needn't handle non-finite values.
Results may differ from the reference program's by a relative error of at most 0.0095.
Values may be sent and summed in bfloat16 or wider, within the bound.
A program may use at most 64 MiB of HBM per device.

```python
import math
import jax
import jax.numpy as jnp
from jax import lax

NVAR = 5
NT = 256
F = 33
RANK = 16
ELEM_PTS = 64
KINDS = 8
RECORD = 512
NB = 8
PD = 128
NPTS = 4096
ELEMS = 64
N_TM = 16
N_SPACE = 2


def draw_snapshots(key, part):
    key_noise, key_scale = jax.random.split(key, 2)
    point_idx = jnp.arange(NPTS, dtype=jnp.int32)
    tm_pos = (point_idx // PD % N_TM).astype(jnp.float32) / max(N_TM - 1, 1)
    space_pos = (point_idx // (PD * N_TM)).astype(jnp.float32) / max(N_SPACE - 1, 1)
    noise = jax.random.normal(key_noise, (RECORD, NVAR, NPTS), jnp.float32)
    ramp = 1.0 + 1.2 * tm_pos + 0.6 * space_pos
    noise = jnp.clip(noise, -6.0, 6.0)
    spread = jnp.exp(jax.random.uniform(key_scale, (1, NVAR, NPTS), jnp.float32, 0.0, math.log(10.0)))
    return (noise * spread * ramp[None, None, :]).astype(jnp.bfloat16)


def draw_mass_table(key, part):
    key_diag, key_off = jax.random.split(key)
    diagonal = jax.random.uniform(key_diag, (KINDS, ELEM_PTS), jnp.float32, 2.0, 3.0)
    off_part = jax.random.uniform(key_off, (KINDS, ELEM_PTS, ELEM_PTS), jnp.float32, -0.03, 0.03)
    symmetric = 0.5 * (off_part + jnp.swapaxes(off_part, 1, 2))
    position = jnp.arange(ELEM_PTS, dtype=jnp.int32)
    on_diag = position[:, None] == position[None, :]
    return jnp.where(on_diag[None], diagonal[:, :, None], symmetric)


def draw_offsets(key, part):
    key_vals, key_perm = jax.random.split(key)
    values = jax.random.randint(key_vals, (NB,), 0, RECORD - NT + 1, dtype=jnp.int32)
    order = jax.random.permutation(key_perm, NB)
    values = values.at[order[0]].set(0)
    values = values.at[order[1]].set(RECORD - NT)
    return values


def plant(values, rng, least, top_value):
    longest = values.shape.index(max(values.shape))
    spots = []
    for shift in (0, 1):
        where = [jax.random.randint(jax.random.fold_in(rng, axis), (), 0, length) for axis, length in enumerate(values.shape)]
        where[longest] = (where[longest] + shift) % values.shape[longest]
        spots.append(tuple(where))
    return values.at[spots[0]].set(least).at[spots[1]].set(top_value)


def shard_levels(own_key, shape, cuts, smallest, high):
    loudness = 1.0
    for dim, shards_of in cuts:
        draws = jax.random.uniform(jax.random.fold_in(jax.random.fold_in(own_key, 6), dim), (shards_of,), jnp.float32, smallest / len(cuts), high / len(cuts))
        loudness = loudness * jnp.repeat(jnp.exp(draws), shape[dim] // shards_of).reshape((-1,) + (1,) * (len(shape) - 1 - dim))
    return loudness


def centred(rng, extent, scale, reach, cuts=(), held_as=jnp.bfloat16):
    gain = shard_levels(rng, extent, cuts, -0.22, 0.18) if cuts else 1.0
    values = jax.random.normal(rng, extent, jnp.float32) * scale * gain
    return jnp.minimum(jnp.maximum(values, -reach), reach).astype(held_as)


def setup_inputs(seed: int = 0) -> dict:
    key_of = jax.random.split(jax.random.key(seed), 6)
    return {
        "snapshots": draw_snapshots(jax.random.fold_in(key_of[5], 71), 0),
        "basis": centred(key_of[1], (2, F, RANK, NVAR, NPTS), 1.0, 6.0, ((4, 32),)),
        "mass_table": draw_mass_table(jax.random.fold_in(key_of[5], 71), 0),
        "elem_kind": plant(jax.random.randint(key_of[3], (ELEMS,), 0, KINDS), jax.random.fold_in(key_of[3], 1), 0, KINDS - 1).astype(jnp.int32),
        "offsets": draw_offsets(jax.random.fold_in(key_of[5], 71), 0),
    }


def spectral_table(offsets, window_len, freq_count, record_len):
    snap_idx = jnp.arange(record_len, dtype=jnp.int32)
    time_lag = snap_idx[None, :] - offsets[:, None].astype(jnp.int32)
    inside = (time_lag >= 0) & (time_lag < window_len)
    lag_clip = jnp.clip(time_lag, 0, window_len - 1)
    lag_float = lag_clip.astype(jnp.float32)
    hann_wt = 0.5 - 0.5 * jnp.cos(2.0 * math.pi / window_len * lag_float)
    norm_wt = 1.0 / math.sqrt(0.375 * window_len)
    freq_idx = jnp.arange(freq_count, dtype=jnp.int32)
    phase_int = jnp.mod(freq_idx[:, None, None] * lag_clip[None], window_len)
    angle = 2.0 * math.pi / window_len * phase_int.astype(jnp.float32)
    weight = jnp.where(inside, hann_wt * norm_wt, jnp.zeros_like(hann_wt))[None]
    real_part = weight * jnp.cos(angle)
    imag_part = -weight * jnp.sin(angle)
    return jnp.stack([real_part, imag_part]).astype(jnp.bfloat16)

def apply_mass(field, mass_blk):
    lead = field.shape[:-1]
    elem_count = mass_blk.shape[0]
    shaped = field.reshape(lead + (elem_count, ELEM_PTS))
    result = jnp.einsum('...ep,epq->...eq', shaped, mass_blk, precision=lax.Precision.HIGHEST)
    return result.reshape(field.shape)

def project(mode_rows, weighted):
    real_out = jnp.einsum('fkx,fbx->fbk', mode_rows[0], weighted[0]) + jnp.einsum('fkx,fbx->fbk', mode_rows[1], weighted[1])
    imag_out = jnp.einsum('fkx,fbx->fbk', mode_rows[0], weighted[1]) - jnp.einsum('fkx,fbx->fbk', mode_rows[1], weighted[0])
    return jnp.stack([real_out, imag_out])

def time_kernel(dft_table, coeffs):
    table_f = dft_table.astype(jnp.float32)
    coeff_round = lax.optimization_barrier(coeffs.astype(jnp.bfloat16)).astype(jnp.float32)
    real_out = jnp.einsum('fbt,fbk->fkt', table_f[0], coeff_round[0]) - jnp.einsum('fbt,fbk->fkt', table_f[1], coeff_round[1])
    imag_out = jnp.einsum('fbt,fbk->fkt', table_f[0], coeff_round[1]) + jnp.einsum('fbt,fbk->fkt', table_f[1], coeff_round[0])
    return jnp.stack([real_out, imag_out]).astype(jnp.bfloat16)

def reference(snapshots, basis, mass_table, elem_kind, offsets):
    dft_table = spectral_table(offsets, NT, F, RECORD)
    table_flat = dft_table.reshape(2 * F * NB, RECORD)
    entries = NVAR * NPTS
    block_pts = math.gcd(NPTS, 4096)
    block_count = NPTS // block_pts
    block_elems = block_pts // ELEM_PTS
    block_ids = jnp.arange(block_count, dtype=jnp.int32)

    def block_data(block_index):
        first_pt = (block_index * block_pts).astype(jnp.int32)
        record_blk = lax.dynamic_slice_in_dim(snapshots, first_pt, block_pts, 2)
        kinds_blk = lax.dynamic_slice_in_dim(elem_kind, (block_index * block_elems).astype(jnp.int32), block_elems, 0)
        mass_blk = mass_table[kinds_blk]
        return (record_blk.reshape(RECORD, NVAR * block_pts), mass_blk, first_pt)

    def coefficient_part(block_index):
        record_flat, mass_blk, first_pt = block_data(block_index)
        basis_blk = lax.dynamic_slice_in_dim(basis, first_pt, block_pts, 4)
        spectra = jnp.dot(table_flat, record_flat, preferred_element_type=jnp.float32)
        weighted = apply_mass(spectra.reshape(2, F, NB, NVAR, block_pts), mass_blk).astype(jnp.bfloat16)
        weighted = weighted.reshape(2, F, NB, NVAR * block_pts).astype(jnp.float32)
        mode_rows = basis_blk.reshape(2, F, RANK, NVAR * block_pts).astype(jnp.float32)
        return project(mode_rows, weighted)
    coeffs = lax.optimization_barrier(jnp.sum(lax.map(coefficient_part, block_ids), axis=0)) / math.sqrt(entries)
    kernel = time_kernel(dft_table, coeffs).reshape(2 * F * RANK, RECORD)

    def field_block(block_index):
        record_flat, mass_blk, first_pt = block_data(block_index)
        fields = jnp.dot(kernel, record_flat, preferred_element_type=jnp.float32)
        return (fields.reshape(2, F, RANK, NVAR, block_pts), mass_blk)

    def energy_part(block_index):
        fields, mass_blk = field_block(block_index)
        massed = apply_mass(fields, mass_blk)
        return lax.optimization_barrier(jnp.sum(fields * massed, axis=(0, 3, 4)))
    energy = lax.optimization_barrier(jnp.sum(lax.map(energy_part, block_ids), axis=0))
    factor = 1.0 / jnp.sqrt(energy / entries + 1e-06)

    def output_part(block_index):
        fields, mass_blk = field_block(block_index)
        return (fields * factor[None, :, :, None, None]).astype(jnp.bfloat16)
    pieces = lax.map(output_part, block_ids)
    new_basis = jnp.moveaxis(pieces, 0, 4).reshape(2, F, RANK, NVAR, NPTS)
    return (coeffs, new_basis)
```

```python
import functools
import math

import jax
import jax.numpy as jnp
from jax import lax
from jax.experimental import pallas as pl
from jax.experimental.pallas import tpu as pltpu
from jax.sharding import PartitionSpec as P

NT = 256
GROUP = 8
MESH = pl.DeviceIdType.MESH
BF = jnp.bfloat16
F32 = jnp.float32


def mm(a, b, contract):
    return lax.dot_general(a, b, (contract, ((), ())), preferred_element_type=F32)


def kernel(
    n_tm, n_sp, entries,
    snap, basis, mass, kinds, offs,
    coef_out, new_out,
    table, rec, ub, sh, wt, xb, slots, yb, ob,
    a_send, a_recv, b_sem, s1, r1, s2, r2, o_sem,
):
    n = n_tm * n_sp
    tm = lax.axis_index("tm")
    sp = lax.axis_index("space")
    me = sp * n_tm + tm
    freqs = basis.shape[1]
    nvar, rows, pts = rec.shape[1:]
    groups = sh.shape[0] // (2 * GROUP * 8)
    record = n_tm * rows
    blocks = offs.shape[0]
    modes = basis.shape[3]
    upo = slots.shape[1]
    owners = xb.shape[0] // upo
    half = GROUP * blocks
    lanes = GROUP * modes

    def device(d):
        return {"tm": lax.rem(d, n_tm), "space": lax.div(d, n_tm)}

    barrier = pltpu.get_barrier_semaphore()

    def greet(i, carry):
        pl.semaphore_signal(barrier, inc=1, device_id=device(lax.rem(me + i, n)), device_id_type=MESH)
        return carry

    lax.fori_loop(1, n, greet, 0)
    load_basis = pltpu.make_async_copy(basis, ub.at[:, pl.ds(0, freqs)], b_sem)
    load_basis.start()
    pl.semaphore_wait(barrier, n - 1)

    def send(i, carry):
        to = lax.rem(tm + i, n_tm)
        pltpu.make_async_remote_copy(
            snap.at[:, :, pl.ds(pl.multiple_of(to * pts, pts), pts)],
            rec.at[tm], a_send, a_recv, device_id={"tm": to, "space": sp}, device_id_type=MESH,
        ).start()
        return carry

    lax.fori_loop(1, n_tm, send, 0)
    pltpu.make_async_copy(
        snap.at[:, :, pl.ds(pl.multiple_of(tm * pts, pts), pts)], rec.at[tm], a_recv
    ).start()

    row = lax.broadcasted_iota(jnp.int32, (blocks, record), 0)
    lag = lax.broadcasted_iota(jnp.int32, (blocks, record), 1)
    for b in range(blocks):
        lag = jnp.where(row == b, lag - offs[b], lag)
    inside = (lag >= 0) & (lag < NT)
    theta = jnp.clip(lag, 0, NT - 1).astype(F32) * (2.0 * math.pi / NT)
    c1, s1v = jnp.cos(theta), jnp.sin(theta)
    win = jnp.where(inside, (0.5 - 0.5 * c1) * (1.0 / math.sqrt(0.375 * NT)), 0.0)
    cc, ss = win, jnp.zeros_like(win)
    for f in range(0, groups * GROUP, 2):
        c_next, s_next = cc * c1 - ss * s1v, ss * c1 + cc * s1v
        at = (f // GROUP) * 2 * half + (f % GROUP) * blocks
        table[at : at + 2 * blocks] = jnp.concatenate([cc, c_next], axis=0).astype(BF)
        table[at + half : at + half + 2 * blocks] = jnp.concatenate([-ss, -s_next], axis=0).astype(BF)
        cc, ss = c_next * c1 - s_next * s1v, s_next * c1 + c_next * s1v

    size = mass.shape[1]
    elems = pts // size
    strips = []
    for e in range(elems):
        kind = jnp.full((size, size), kinds[e], jnp.int32)
        blk = mass[0]
        for k in range(1, mass.shape[0]):
            blk = jnp.where(kind == k, mass[k], blk)
        zero = jnp.zeros_like(blk)
        strips.append(jnp.concatenate([blk if j == e else zero for j in range(elems)], axis=1))
    m_all = jnp.concatenate(strips, axis=0)
    m_hi = m_all.astype(BF)
    m_lo = (m_all - m_hi.astype(F32)).astype(BF)
    m_stack = jnp.concatenate([m_hi, m_hi, m_lo], axis=0)

    load_basis.wait()
    ub[:, freqs:] = jnp.zeros((2, groups * GROUP - freqs) + ub.shape[2:], BF)

    pltpu.make_async_copy(rec, rec, a_recv).wait()
    x = jnp.concatenate([rec[:, v].reshape(record, pts) for v in range(nvar)], axis=1)
    spec = mm(table[...], x, ((1,), (0,)))
    s_hi = spec.astype(BF)
    s_lo = (spec - s_hi.astype(F32)).astype(BF)
    sh[...] = s_hi
    for v in range(nvar):
        cut = slice(v * pts, (v + 1) * pts)
        lhs = jnp.concatenate([s_hi[:, cut], s_lo[:, cut], s_hi[:, cut]], axis=1)
        wt[:, cut] = mm(lhs, m_stack, ((1,), (0,))).astype(BF)

    row_f = lax.broadcasted_iota(jnp.int32, (GROUP, blocks, lanes), 0)
    lane = lax.broadcasted_iota(jnp.int32, (GROUP, blocks, lanes), 2)
    diag_k = row_f == lane // modes
    diag_b = row_f == (lane % half) // blocks
    lane2 = lax.broadcasted_iota(jnp.int32, (blocks, lanes), 1)

    def fold(full, mask):
        return jnp.sum(jnp.where(mask, full.reshape(GROUP, blocks, lanes), 0.0), axis=0)

    def put(i, val):
        h = blocks // 2
        xb[2 * i] = val[:h]
        xb[2 * i + 1] = val[h:]

    def get(i):
        return jnp.concatenate([yb[2 * i], yb[2 * i + 1]], axis=0)

    for g in range(groups):
        top = g * 2 * half
        w_g = wt[top : top + 2 * half]
        f0 = g * GROUP
        u = [
            jnp.concatenate(
                [ub[c, f0 : f0 + GROUP, v].reshape(lanes, pts) for v in range(nvar)], axis=1
            )
            for c in range(2)
        ]
        lhs = jnp.concatenate(u + [sh[top : top + 2 * half]], axis=0)
        full = mm(w_g, lhs, ((1,), (1,)))
        rr = fold(full[:half, :lanes], diag_k)
        ri = fold(full[:half, lanes : 2 * lanes], diag_k)
        ir = fold(full[half:, :lanes], diag_k)
        ii = fold(full[half:, lanes : 2 * lanes], diag_k)
        p_r = fold(full[:half, 2 * lanes :], diag_b)
        p_i = pltpu.roll(fold(full[half:, 2 * lanes :], diag_b), half, 1)
        put(3 * g, rr + ii)
        put(3 * g + 1, ir - ri)
        put(3 * g + 2, jnp.where(lane2 < half, p_r + p_i, p_i - p_r))

    def scatter(i, carry):
        o = lax.rem(me + i, owners)

        @pl.when(o != me)
        def _():
            pltpu.make_async_remote_copy(
                xb.at[pl.ds(o * upo, upo)], slots.at[me], s1, r1,
                device_id=device(o), device_id_type=MESH,
            ).start()

        return carry

    lax.fori_loop(0, owners, scatter, 0)

    @pl.when(me < owners)
    def _():
        pltpu.make_async_copy(xb.at[pl.ds(me * upo, upo)], slots.at[me], r1).start()
        pltpu.make_async_copy(slots, slots, r1).wait()
        yb[pl.ds(me * upo, upo)] = jnp.sum(slots[...], axis=0)

        def spread(i, carry):
            pltpu.make_async_remote_copy(
                yb.at[pl.ds(me * upo, upo)], yb.at[pl.ds(me * upo, upo)], s2, r2,
                device_id=device(lax.rem(me + i, n)), device_id_type=MESH,
            ).start()
            return carry

        lax.fori_loop(1, n, spread, 0)
        part = yb.at[pl.ds(0, (owners - 1) * upo)]
        pltpu.make_async_copy(part, part, r2).wait()

    @pl.when(me >= owners)
    def _():
        pltpu.make_async_copy(yb, yb, r2).wait()

    scale = 1.0 / math.sqrt(entries)
    outs = []
    for g in range(groups):
        top = g * 2 * half
        f0 = g * GROUP
        nf = min(GROUP, freqs - f0)
        co_r, co_i = get(3 * g) * scale, get(3 * g + 1) * scale
        coef_out[0, g] = co_r
        coef_out[1, g] = co_i
        cr = co_r.astype(BF).astype(F32)
        ci = co_i.astype(BF).astype(F32)
        gram = get(3 * g + 2)

        def spread_rows(val, mask):
            big = jnp.broadcast_to(val[None], (GROUP, blocks, lanes))
            return jnp.where(mask, big, 0.0).reshape(half, lanes)

        d_r, d_i = spread_rows(cr, diag_k), spread_rows(ci, diag_k)
        turned = pltpu.roll(gram, half, 1)
        turned = jnp.where(lane2 < half, -turned, turned)
        quad = jnp.concatenate([spread_rows(gram, diag_b), spread_rows(turned, diag_b)], axis=0)
        vec = jnp.concatenate([d_r, d_i], axis=0)
        energy = jnp.sum(vec * mm(quad.astype(BF), vec.astype(BF), ((1,), (0,))), axis=0, keepdims=True)
        factor = 1.0 / jnp.sqrt(energy / entries + 1e-06)
        fac = jnp.transpose(jnp.broadcast_to(factor, (pts, lanes)))
        s_g = sh[top : top + 2 * half]
        for c in range(2):
            d = jnp.concatenate([d_r, -d_i] if c == 0 else [d_i, d_r], axis=0)
            field = mm(jnp.transpose(d).astype(BF), s_g, ((1,), (0,)))
            for v in range(nvar):
                val = (field[:, v * pts : (v + 1) * pts] * fac).astype(BF).reshape(GROUP, modes, pts)
                ob[c, f0 : f0 + nf, v] = val[:nf]
        cp = pltpu.make_async_copy(ob.at[:, pl.ds(f0, nf)], new_out.at[:, pl.ds(f0, nf)], o_sem.at[g])
        cp.start()
        outs.append(cp)

    for cp in outs:
        cp.wait()
    first = rec.at[pl.ds(0, n_tm - 1)]
    pltpu.make_async_copy(first, first, a_send).wait()

    @pl.when(me < owners)
    def _():
        part = xb.at[pl.ds(0, (owners - 1) * upo)]
        pltpu.make_async_copy(part, part, s1).wait()
        whole = slots.at[pl.ds(0, n - 1)]
        pltpu.make_async_copy(whole, whole, s2).wait()

    @pl.when(me >= owners)
    def _():
        pltpu.make_async_copy(xb, xb, s1).wait()


def solution(mesh):
    n_tm, n_sp = mesh.shape["tm"], mesh.shape["space"]
    n = n_tm * n_sp

    def on_device(snapshots, basis, mass_table, elem_kind, offsets):
        rows, nvar, slab = snapshots.shape
        _, freqs, modes, _, pts = basis.shape
        blocks = offsets.shape[0]
        groups = -(-freqs // GROUP)
        entries = nvar * pts * n
        units = 6 * groups
        upo = -(-units // n)
        owners = -(-units // upo)
        table_rows = groups * 2 * GROUP * blocks
        unit = (blocks // 2, GROUP * modes)
        snap = jnp.transpose(snapshots, (1, 0, 2))
        base = jnp.transpose(basis, (0, 1, 3, 2, 4))
        any_spec = pl.BlockSpec(memory_space=pl.ANY)
        vmem = pl.BlockSpec(memory_space=pltpu.VMEM)
        smem = pl.BlockSpec(memory_space=pltpu.SMEM)
        coef, new = pl.pallas_call(
            functools.partial(kernel, n_tm, n_sp, entries),
            out_shape=(
                jax.ShapeDtypeStruct((2, groups, blocks, GROUP * modes), F32),
                jax.ShapeDtypeStruct(base.shape, BF),
            ),
            in_specs=[any_spec, any_spec, vmem, smem, smem],
            out_specs=(vmem, any_spec),
            scratch_shapes=[
                pltpu.VMEM((table_rows, rows * n_tm), BF),
                pltpu.VMEM((n_tm, nvar, rows, pts), BF),
                pltpu.VMEM((2, groups * GROUP, nvar, modes, pts), BF),
                pltpu.VMEM((table_rows, nvar * pts), BF),
                pltpu.VMEM((table_rows, nvar * pts), BF),
                pltpu.VMEM((owners * upo,) + unit, F32),
                pltpu.VMEM((n, upo) + unit, F32),
                pltpu.VMEM((owners * upo,) + unit, F32),
                pltpu.VMEM((2, freqs, nvar, modes, pts), BF),
            ]
            + [pltpu.SemaphoreType.DMA] * 7
            + [pltpu.SemaphoreType.DMA((groups,))],
            compiler_params=pltpu.CompilerParams(
                collective_id=0, has_side_effects=True, vmem_limit_bytes=48 * 1024 * 1024
            ),
        )(snap, base, mass_table, elem_kind, offsets)
        coef = coef.reshape(2, groups, blocks, GROUP, modes).transpose(0, 1, 3, 2, 4)
        coef = coef.reshape(2, groups * GROUP, blocks, modes)[:, :freqs]
        return coef, jnp.transpose(new, (0, 1, 3, 2, 4))

    return jax.shard_map(
        on_device,
        mesh=mesh,
        in_specs=(
            P("tm", None, "space"),
            P(None, None, None, None, ("space", "tm")),
            P(),
            P(("space", "tm")),
            P(),
        ),
        out_specs=(P(), P(None, None, None, None, ("space", "tm"))),
        check_vma=False,
    )
```

```python
import functools
import math

import jax
import jax.numpy as jnp
from jax import lax
from jax.experimental import pallas as pl
from jax.experimental.pallas import tpu as pltpu
from jax.sharding import PartitionSpec as P

NT = 256
GROUP = 8
MESH = pl.DeviceIdType.MESH
BF = jnp.bfloat16
F32 = jnp.float32


def mm(a, b, contract):
    return lax.dot_general(a, b, (contract, ((), ())), preferred_element_type=F32)


def kernel(
    n_tm, n_sp, low, entries, chunks,
    snap, basis, mass_in, kinds_in, offs_in,
    coef_out, new_out,
    table, ub, sh, xb, line, plane, yb, mass, kinds, offs, *rest,
):
    recs, (a_send, a_recv, l_sem, s1, r1, s2, r2, s3, r3) = rest[: len(chunks)], rest[len(chunks) :]
    tm = lax.axis_index("tm")
    sp = lax.axis_index("space")
    high = n_tm // low
    side = low * n_sp
    spot = sp * low + lax.rem(tm, low)
    level = lax.div(tm, low)
    freqs = basis.shape[1]
    rows, pts = recs[0].shape[2:]
    groups = sh.shape[0] // (2 * GROUP * 8)
    record = n_tm * rows
    blocks = offs.shape[0]
    modes = basis.shape[3]
    upo = plane.shape[1]
    owners = xb.shape[0] // upo
    half = GROUP * blocks
    lanes = GROUP * modes

    def beside(p):
        return {"tm": level * low + lax.rem(p, low), "space": lax.div(p, low)}

    barrier = pltpu.get_barrier_semaphore()

    def greet_line(i, carry):
        pl.semaphore_signal(
            barrier, inc=1, device_id={"tm": lax.rem(tm + i, n_tm), "space": sp}, device_id_type=MESH
        )
        return carry

    def greet_side(i, carry):
        to = lax.rem(sp + lax.div(i, low), n_sp)
        pl.semaphore_signal(
            barrier, inc=1, device_id={"tm": level * low + lax.rem(i, low), "space": to}, device_id_type=MESH
        )
        return carry

    lax.fori_loop(1, n_tm, greet_line, 0)
    lax.fori_loop(low, side, greet_side, 0)
    loads = [
        pltpu.make_async_copy(offs_in, offs, l_sem.at[0]),
        pltpu.make_async_copy(kinds_in, kinds, l_sem.at[1]),
        pltpu.make_async_copy(mass_in, mass, l_sem.at[2]),
        pltpu.make_async_copy(basis, ub.at[:, pl.ds(0, freqs)], l_sem.at[3]),
    ]
    for cp in loads:
        cp.start()
    pl.semaphore_wait(barrier, n_tm - 1 + side - low)

    for ci, (v0, v1) in enumerate(chunks):

        def block(to):
            return snap.at[pl.ds(v0, v1 - v0), :, pl.ds(pl.multiple_of(to * pts, pts), pts)]

        def send(i, carry):
            d = lax.div(i + 1, 2)
            to = lax.rem(tm + n_tm // 2 + jnp.where(lax.rem(i, 2) == 0, d, -d) + n_tm, n_tm)
            pltpu.make_async_remote_copy(
                block(to), recs[ci].at[tm], a_send.at[ci], a_recv.at[ci],
                device_id={"tm": to, "space": sp}, device_id_type=MESH,
            ).start()
            return carry

        lax.fori_loop(0, n_tm - 1, send, 0)
        pltpu.make_async_copy(block(tm), recs[ci].at[tm], a_recv.at[ci]).start()

    loads[0].wait()
    row = lax.broadcasted_iota(jnp.int32, (blocks, record), 0)
    lag = lax.broadcasted_iota(jnp.int32, (blocks, record), 1)
    for b in range(blocks):
        lag = jnp.where(row == b, lag - offs[b], lag)
    inside = (lag >= 0) & (lag < NT)
    theta = jnp.clip(lag, 0, NT - 1).astype(F32) * (2.0 * math.pi / NT)
    c1, s1v = jnp.cos(theta), jnp.sin(theta)
    win = jnp.where(inside, (0.5 - 0.5 * c1) * (1.0 / math.sqrt(0.375 * NT)), 0.0)
    cc, ss = win, jnp.zeros_like(win)
    for f in range(0, groups * GROUP, 2):
        c_next, s_next = cc * c1 - ss * s1v, ss * c1 + cc * s1v
        at = (f // GROUP) * 2 * half + (f % GROUP) * blocks
        table[at : at + 2 * blocks] = jnp.concatenate([cc, c_next], axis=0).astype(BF)
        table[at + half : at + half + 2 * blocks] = jnp.concatenate([-ss, -s_next], axis=0).astype(BF)
        cc, ss = c_next * c1 - s_next * s1v, s_next * c1 + c_next * s1v

    loads[1].wait()
    loads[2].wait()
    size = mass.shape[1]
    elems = pts // size
    strips = []
    for e in range(elems):
        kind = jnp.full((size, size), kinds[e], jnp.int32)
        blk = mass[0]
        for k in range(1, mass.shape[0]):
            blk = jnp.where(kind == k, mass[k], blk)
        zero = jnp.zeros_like(blk)
        strips.append(jnp.concatenate([blk if j == e else zero for j in range(elems)], axis=1))
    m_all = jnp.concatenate(strips, axis=0)
    m_hi = m_all.astype(BF)
    m_lo = (m_all - m_hi.astype(F32)).astype(BF)
    m_stack = jnp.concatenate([m_hi, m_hi, m_lo], axis=0)

    loads[3].wait()
    ub[:, freqs:] = jnp.zeros((2, groups * GROUP - freqs) + ub.shape[2:], BF)

    row_f = lax.broadcasted_iota(jnp.int32, (GROUP, blocks, lanes), 0)
    lane = lax.broadcasted_iota(jnp.int32, (GROUP, blocks, lanes), 2)
    diag_k = row_f == lane // modes
    diag_b = row_f == (lane % half) // blocks
    lane2 = lax.broadcasted_iota(jnp.int32, (blocks, lanes), 1)

    def fold(full, mask):
        return jnp.sum(jnp.where(mask, full.reshape(GROUP, blocks, lanes), 0.0), axis=0)

    total = [None] * (3 * groups)
    for ci, (v0, v1) in enumerate(chunks):
        rec = recs[ci]
        pltpu.make_async_copy(rec, rec, a_recv.at[ci]).wait()
        count = v1 - v0
        x = jnp.concatenate([rec[:, v].reshape(record, pts) for v in range(count)], axis=1)
        spec = mm(table[...], x, ((1,), (0,)))
        s_hi = spec.astype(BF)
        s_lo = (spec - s_hi.astype(F32)).astype(BF)
        sh[:, v0 * pts : v1 * pts] = s_hi
        wts = []
        for v in range(count):
            cut = slice(v * pts, (v + 1) * pts)
            lhs = jnp.concatenate([s_hi[:, cut], s_lo[:, cut], s_hi[:, cut]], axis=1)
            wts.append(mm(lhs, m_stack, ((1,), (0,))).astype(BF))
        wt = jnp.concatenate(wts, axis=1)
        for g in range(groups):
            top = g * 2 * half
            f0 = g * GROUP
            u = [
                jnp.concatenate(
                    [ub[c, f0 : f0 + GROUP, v].reshape(lanes, pts) for v in range(v0, v1)], axis=1
                )
                for c in range(2)
            ]
            lhs = jnp.concatenate(u + [s_hi[top : top + 2 * half]], axis=0)
            full = mm(wt[top : top + 2 * half], lhs, ((1,), (1,)))
            rr = fold(full[:half, :lanes], diag_k)
            ri = fold(full[:half, lanes : 2 * lanes], diag_k)
            ir = fold(full[half:, :lanes], diag_k)
            ii = fold(full[half:, lanes : 2 * lanes], diag_k)
            p_r = fold(full[:half, 2 * lanes :], diag_b)
            p_i = pltpu.roll(fold(full[half:, 2 * lanes :], diag_b), half, 1)
            new = [rr + ii, ir - ri, jnp.where(lane2 < half, p_r + p_i, p_i - p_r)]
            for j in range(3):
                at = 3 * g + j
                total[at] = new[j] if ci == 0 else total[at] + new[j]
    for at in range(3 * groups):
        xb[at] = total[at]

    mine = pl.ds(spot * upo, upo)

    def scatter(i, carry):
        o = lax.rem(spot + i, owners)

        @pl.when(o != spot)
        def _():
            pltpu.make_async_remote_copy(
                xb.at[pl.ds(o * upo, upo)], plane.at[spot], s1, r1,
                device_id=beside(o), device_id_type=MESH,
            ).start()

        return carry

    lax.fori_loop(0, owners, scatter, 0)

    def wait_bytes(ref, sem):
        pltpu.make_async_copy(ref, ref, sem).wait()

    @pl.when(spot < owners)
    def _():
        plane[spot] = xb[mine]
        wait_bytes(plane.at[pl.ds(0, side - 1)], r1)
        line[level] = jnp.sum(plane[...], axis=0)

        def exchange(i, carry):
            to = lax.rem(level + i, high) * low + lax.rem(tm, low)
            pltpu.make_async_remote_copy(
                line.at[level], line.at[level], s2, r2,
                device_id={"tm": to, "space": sp}, device_id_type=MESH,
            ).start()
            return carry

        if high > 1:
            lax.fori_loop(1, high, exchange, 0)
            wait_bytes(line.at[pl.ds(0, high - 1)], r2)
        yb[mine] = jnp.sum(line[...], axis=0)

        def gather(i, carry):
            pltpu.make_async_remote_copy(
                yb.at[mine], yb.at[mine], s3, r3,
                device_id=beside(lax.rem(spot + i, side)), device_id_type=MESH,
            ).start()
            return carry

        lax.fori_loop(1, side, gather, 0)
        wait_bytes(yb.at[pl.ds(0, (owners - 1) * upo)], r3)

    @pl.when(spot >= owners)
    def _():
        wait_bytes(yb, r3)

    scale = 1.0 / math.sqrt(entries)
    nvar = sh.shape[1] // pts
    for g in range(groups):
        top = g * 2 * half
        f0 = g * GROUP
        nf = min(GROUP, freqs - f0)
        co_r, co_i = yb[3 * g] * scale, yb[3 * g + 1] * scale
        coef_out[0, g] = co_r
        coef_out[1, g] = co_i
        cr = co_r.astype(BF).astype(F32)
        ci = co_i.astype(BF).astype(F32)
        gram = yb[3 * g + 2]

        def spread_rows(val, mask):
            big = jnp.broadcast_to(val[None], (GROUP, blocks, lanes))
            return jnp.where(mask, big, 0.0).reshape(half, lanes)

        d_r, d_i = spread_rows(cr, diag_k), spread_rows(ci, diag_k)
        turned = pltpu.roll(gram, half, 1)
        turned = jnp.where(lane2 < half, -turned, turned)
        quad = jnp.concatenate([spread_rows(gram, diag_b), spread_rows(turned, diag_b)], axis=0)
        vec = jnp.concatenate([d_r, d_i], axis=0)
        energy = jnp.sum(vec * mm(quad.astype(BF), vec.astype(BF), ((1,), (0,))), axis=0, keepdims=True)
        factor = 1.0 / jnp.sqrt(energy / entries + 1e-06)
        fac = jnp.transpose(jnp.broadcast_to(factor, (pts, lanes)))
        s_g = sh[top : top + 2 * half]
        for c in range(2):
            d = jnp.concatenate([d_r, -d_i] if c == 0 else [d_i, d_r], axis=0)
            field = mm(jnp.transpose(d).astype(BF), s_g, ((1,), (0,)))
            for v in range(nvar):
                val = (field[:, v * pts : (v + 1) * pts] * fac).astype(BF).reshape(GROUP, modes, pts)
                new_out[c, f0 : f0 + nf, v] = val[:nf]

    for ci in range(len(chunks)):
        wait_bytes(recs[ci].at[pl.ds(0, n_tm - 1)], a_send.at[ci])

    @pl.when(spot < owners)
    def _():
        wait_bytes(xb.at[pl.ds(0, (owners - 1) * upo)], s1)
        if high > 1:
            wait_bytes(line.at[pl.ds(0, high - 1)], s2)
        wait_bytes(plane.at[pl.ds(0, side - 1)], s3)

    @pl.when(spot >= owners)
    def _():
        wait_bytes(xb, s1)


def solution(mesh):
    n_tm, n_sp = mesh.shape["tm"], mesh.shape["space"]
    n = n_tm * n_sp

    def on_device(snapshots, basis, mass_table, elem_kind, offsets):
        rows, nvar, slab = snapshots.shape
        _, freqs, modes, _, pts = basis.shape
        blocks = offsets.shape[0]
        groups = -(-freqs // GROUP)
        entries = nvar * pts * n
        units = 3 * groups
        low = math.gcd(n_tm, 4)
        side = low * n_sp
        upo = -(-units // side)
        owners = -(-units // upo)
        table_rows = groups * 2 * GROUP * blocks
        unit = (blocks, GROUP * modes)
        chunks = tuple((v, min(v + 2, nvar)) for v in range(0, nvar, 2))
        snap = jnp.transpose(snapshots, (1, 0, 2))
        base = jnp.transpose(basis, (0, 1, 3, 2, 4))
        hbm = pl.BlockSpec(memory_space=pltpu.HBM)
        vmem = pl.BlockSpec(memory_space=pltpu.VMEM)
        coef, new = pl.pallas_call(
            functools.partial(kernel, n_tm, n_sp, low, entries, chunks),
            out_shape=(
                jax.ShapeDtypeStruct((2, groups, blocks, GROUP * modes), F32),
                jax.ShapeDtypeStruct(base.shape, BF),
            ),
            in_specs=[hbm] * 5,
            out_specs=(vmem, vmem),
            scratch_shapes=[
                pltpu.VMEM((table_rows, rows * n_tm), BF),
                pltpu.VMEM((2, groups * GROUP, nvar, modes, pts), BF),
                pltpu.VMEM((table_rows, nvar * pts), BF),
                pltpu.VMEM((owners * upo,) + unit, F32),
                pltpu.VMEM((n_tm // low, upo) + unit, F32),
                pltpu.VMEM((side, upo) + unit, F32),
                pltpu.VMEM((owners * upo,) + unit, F32),
                pltpu.VMEM(mass_table.shape, F32),
                pltpu.SMEM(elem_kind.shape, jnp.int32),
                pltpu.SMEM(offsets.shape, jnp.int32),
            ]
            + [pltpu.VMEM((n_tm, v1 - v0, rows, pts), BF) for v0, v1 in chunks]
            + [
                pltpu.SemaphoreType.DMA((len(chunks),)),
                pltpu.SemaphoreType.DMA((len(chunks),)),
                pltpu.SemaphoreType.DMA((4,)),
            ]
            + [pltpu.SemaphoreType.DMA] * 6,
            compiler_params=pltpu.CompilerParams(
                collective_id=0, has_side_effects=True, vmem_limit_bytes=48 * 1024 * 1024
            ),
        )(*[pltpu.with_memory_space_constraint(a, pltpu.HBM) for a in (snap, base, mass_table, elem_kind, offsets)])
        coef = coef.reshape(2, groups, blocks, GROUP, modes).transpose(0, 1, 3, 2, 4)
        coef = coef.reshape(2, groups * GROUP, blocks, modes)[:, :freqs]
        return coef, jnp.transpose(new, (0, 1, 3, 2, 4))

    return jax.shard_map(
        on_device,
        mesh=mesh,
        in_specs=(
            P("tm", None, "space"),
            P(None, None, None, None, ("space", "tm")),
            P(),
            P(("space", "tm")),
            P(),
        ),
        out_specs=(P(), P(None, None, None, None, ("space", "tm"))),
        check_vma=False,
    )
```

```python
import functools
import math

import jax
import jax.numpy as jnp
from jax import lax
from jax.experimental import pallas as pl
from jax.experimental.pallas import tpu as pltpu
from jax.sharding import PartitionSpec as P

NT = 256
GROUP = 8
MESH = pl.DeviceIdType.MESH
BF = jnp.bfloat16
F32 = jnp.float32


def mm(a, b, contract):
    return lax.dot_general(a, b, (contract, ((), ())), preferred_element_type=F32)


def kernel(
    n_tm, n_sp, low, entries, chunks,
    snap, basis, mass_in, kinds_in, offs_in,
    sh, y_out,
    table, ub, xb, line, plane, yb, mass, kinds, offs, *rest,
):
    recs, (a_send, a_recv, l_sem, s1, r1, s2, r2, s3, r3) = rest[: len(chunks)], rest[len(chunks) :]
    tm = lax.axis_index("tm")
    sp = lax.axis_index("space")
    high = n_tm // low
    side = low * n_sp
    spot = sp * low + lax.rem(tm, low)
    level = lax.div(tm, low)
    freqs = basis.shape[1]
    rows, pts = recs[0].shape[2:]
    groups = sh.shape[0] // (2 * GROUP * 8)
    record = n_tm * rows
    blocks = offs.shape[0]
    modes = basis.shape[3]
    upo = plane.shape[1]
    owners = xb.shape[0] // upo
    half = GROUP * blocks
    lanes = GROUP * modes

    def beside(p):
        return {"tm": level * low + lax.rem(p, low), "space": lax.div(p, low)}

    barrier = pltpu.get_barrier_semaphore()

    def greet_line(i, carry):
        pl.semaphore_signal(
            barrier, inc=1, device_id={"tm": lax.rem(tm + i, n_tm), "space": sp}, device_id_type=MESH
        )
        return carry

    def greet_side(i, carry):
        to = lax.rem(sp + lax.div(i, low), n_sp)
        pl.semaphore_signal(
            barrier, inc=1, device_id={"tm": level * low + lax.rem(i, low), "space": to}, device_id_type=MESH
        )
        return carry

    lax.fori_loop(1, n_tm, greet_line, 0)
    lax.fori_loop(low, side, greet_side, 0)
    loads = [
        pltpu.make_async_copy(offs_in, offs, l_sem.at[0]),
        pltpu.make_async_copy(kinds_in, kinds, l_sem.at[1]),
        pltpu.make_async_copy(mass_in, mass, l_sem.at[2]),
        pltpu.make_async_copy(basis, ub.at[:, pl.ds(0, freqs)], l_sem.at[3]),
    ]
    for cp in loads:
        cp.start()
    pl.semaphore_wait(barrier, n_tm - 1 + side - low)

    for ci, (v0, v1) in enumerate(chunks):

        def block(to):
            return snap.at[pl.ds(v0, v1 - v0), :, pl.ds(pl.multiple_of(to * pts, pts), pts)]

        def send(i, carry):
            d = lax.div(i + 1, 2)
            to = lax.rem(tm + n_tm // 2 + jnp.where(lax.rem(i, 2) == 0, d, -d) + n_tm, n_tm)
            pltpu.make_async_remote_copy(
                block(to), recs[ci].at[tm], a_send.at[ci], a_recv.at[ci],
                device_id={"tm": to, "space": sp}, device_id_type=MESH,
            ).start()
            return carry

        lax.fori_loop(0, n_tm - 1, send, 0)
        pltpu.make_async_copy(block(tm), recs[ci].at[tm], a_recv.at[ci]).start()

    loads[0].wait()
    row = lax.broadcasted_iota(jnp.int32, (blocks, record), 0)
    lag = lax.broadcasted_iota(jnp.int32, (blocks, record), 1)
    for b in range(blocks):
        lag = jnp.where(row == b, lag - offs[b], lag)
    inside = (lag >= 0) & (lag < NT)
    theta = jnp.clip(lag, 0, NT - 1).astype(F32) * (2.0 * math.pi / NT)
    c1, s1v = jnp.cos(theta), jnp.sin(theta)
    win = jnp.where(inside, (0.5 - 0.5 * c1) * (1.0 / math.sqrt(0.375 * NT)), 0.0)
    cc, ss = win, jnp.zeros_like(win)
    for f in range(0, groups * GROUP, 2):
        c_next, s_next = cc * c1 - ss * s1v, ss * c1 + cc * s1v
        at = (f // GROUP) * 2 * half + (f % GROUP) * blocks
        table[at : at + 2 * blocks] = jnp.concatenate([cc, c_next], axis=0).astype(BF)
        table[at + half : at + half + 2 * blocks] = jnp.concatenate([-ss, -s_next], axis=0).astype(BF)
        cc, ss = c_next * c1 - s_next * s1v, s_next * c1 + c_next * s1v

    loads[1].wait()
    loads[2].wait()
    size = mass.shape[1]
    elems = pts // size
    strips = []
    for e in range(elems):
        kind = jnp.full((size, size), kinds[e], jnp.int32)
        blk = mass[0]
        for k in range(1, mass.shape[0]):
            blk = jnp.where(kind == k, mass[k], blk)
        zero = jnp.zeros_like(blk)
        strips.append(jnp.concatenate([blk if j == e else zero for j in range(elems)], axis=1))
    m_all = jnp.concatenate(strips, axis=0)
    m_hi = m_all.astype(BF)
    m_lo = (m_all - m_hi.astype(F32)).astype(BF)
    m_stack = jnp.concatenate([m_hi, m_hi, m_lo], axis=0)

    loads[3].wait()
    ub[:, freqs:] = jnp.zeros((2, groups * GROUP - freqs) + ub.shape[2:], BF)

    row_f = lax.broadcasted_iota(jnp.int32, (GROUP, blocks, lanes), 0)
    lane = lax.broadcasted_iota(jnp.int32, (GROUP, blocks, lanes), 2)
    diag_k = row_f == lane // modes
    diag_b = row_f == (lane % half) // blocks
    lane2 = lax.broadcasted_iota(jnp.int32, (blocks, lanes), 1)

    def fold(full, mask):
        return jnp.sum(jnp.where(mask, full.reshape(GROUP, blocks, lanes), 0.0), axis=0)

    total = [None] * (3 * groups)
    for ci, (v0, v1) in enumerate(chunks):
        rec = recs[ci]
        pltpu.make_async_copy(rec, rec, a_recv.at[ci]).wait()
        count = v1 - v0
        x = jnp.concatenate([rec[:, v].reshape(record, pts) for v in range(count)], axis=1)
        spec = mm(table[...], x, ((1,), (0,)))
        s_hi = spec.astype(BF)
        s_lo = (spec - s_hi.astype(F32)).astype(BF)
        sh[:, v0 * pts : v1 * pts] = s_hi
        wts = []
        for v in range(count):
            cut = slice(v * pts, (v + 1) * pts)
            lhs = jnp.concatenate([s_hi[:, cut], s_lo[:, cut], s_hi[:, cut]], axis=1)
            wts.append(mm(lhs, m_stack, ((1,), (0,))).astype(BF))
        wt = jnp.concatenate(wts, axis=1)
        for g in range(groups):
            top = g * 2 * half
            f0 = g * GROUP
            u = [
                jnp.concatenate(
                    [ub[c, f0 : f0 + GROUP, v].reshape(lanes, pts) for v in range(v0, v1)], axis=1
                )
                for c in range(2)
            ]
            lhs = jnp.concatenate(u + [s_hi[top : top + 2 * half]], axis=0)
            full = mm(wt[top : top + 2 * half], lhs, ((1,), (1,)))
            rr = fold(full[:half, :lanes], diag_k)
            ri = fold(full[:half, lanes : 2 * lanes], diag_k)
            ir = fold(full[half:, :lanes], diag_k)
            ii = fold(full[half:, lanes : 2 * lanes], diag_k)
            p_r = fold(full[:half, 2 * lanes :], diag_b)
            p_i = pltpu.roll(fold(full[half:, 2 * lanes :], diag_b), half, 1)
            new = [rr + ii, ir - ri, jnp.where(lane2 < half, p_r + p_i, p_i - p_r)]
            for j in range(3):
                at = 3 * g + j
                total[at] = new[j] if ci == 0 else total[at] + new[j]
    for at in range(3 * groups):
        xb[at] = total[at]

    mine = pl.ds(spot * upo, upo)

    def scatter(i, carry):
        o = lax.rem(spot + i, owners)

        @pl.when(o != spot)
        def _():
            pltpu.make_async_remote_copy(
                xb.at[pl.ds(o * upo, upo)], plane.at[spot], s1, r1,
                device_id=beside(o), device_id_type=MESH,
            ).start()

        return carry

    lax.fori_loop(0, owners, scatter, 0)

    def wait_bytes(ref, sem):
        pltpu.make_async_copy(ref, ref, sem).wait()

    @pl.when(spot < owners)
    def _():
        plane[spot] = xb[mine]
        wait_bytes(plane.at[pl.ds(0, side - 1)], r1)
        line[level] = jnp.sum(plane[...], axis=0)

        def exchange(i, carry):
            to = lax.rem(level + i, high) * low + lax.rem(tm, low)
            pltpu.make_async_remote_copy(
                line.at[level], line.at[level], s2, r2,
                device_id={"tm": to, "space": sp}, device_id_type=MESH,
            ).start()
            return carry

        if high > 1:
            lax.fori_loop(1, high, exchange, 0)
            wait_bytes(line.at[pl.ds(0, high - 1)], r2)
        yb[mine] = jnp.sum(line[...], axis=0)

        def gather(i, carry):
            pltpu.make_async_remote_copy(
                yb.at[mine], yb.at[mine], s3, r3,
                device_id=beside(lax.rem(spot + i, side)), device_id_type=MESH,
            ).start()
            return carry

        lax.fori_loop(1, side, gather, 0)
        wait_bytes(yb.at[pl.ds(0, (owners - 1) * upo)], r3)

    @pl.when(spot >= owners)
    def _():
        wait_bytes(yb, r3)

    y_out[...] = yb[...]
    for ci in range(len(chunks)):
        wait_bytes(recs[ci].at[pl.ds(0, n_tm - 1)], a_send.at[ci])

    @pl.when(spot < owners)
    def _():
        wait_bytes(xb.at[pl.ds(0, (owners - 1) * upo)], s1)
        if high > 1:
            wait_bytes(line.at[pl.ds(0, high - 1)], s2)
        wait_bytes(plane.at[pl.ds(0, side - 1)], s3)

    @pl.when(spot >= owners)
    def _():
        wait_bytes(xb, s1)


def finish(entries, yb, sh, coef_out, new_out, ob, o_sem):
    freqs, nvar, modes, pts = new_out.shape[1:]
    blocks = coef_out.shape[1]
    half = GROUP * blocks
    lanes = GROUP * modes
    groups = -(-freqs // GROUP)
    row_f = lax.broadcasted_iota(jnp.int32, (GROUP, blocks, lanes), 0)
    lane = lax.broadcasted_iota(jnp.int32, (GROUP, blocks, lanes), 2)
    diag_k = row_f == lane // modes
    diag_b = row_f == (lane % half) // blocks
    lane2 = lax.broadcasted_iota(jnp.int32, (blocks, lanes), 1)
    scale = 1.0 / math.sqrt(entries)

    def spread_rows(val, mask):
        big = jnp.broadcast_to(val[None], (GROUP, blocks, lanes))
        return jnp.where(mask, big, 0.0).reshape(half, lanes)

    copies, held = [], []
    for g in range(groups):
        top = g * 2 * half
        f0 = g * GROUP
        nf = min(GROUP, freqs - f0)
        co = [yb[3 * g + c] * scale for c in range(2)]
        held.append(co)
        cr, ci = [v.astype(BF).astype(F32) for v in co]
        gram = yb[3 * g + 2]
        d_r, d_i = spread_rows(cr, diag_k), spread_rows(ci, diag_k)
        turned = pltpu.roll(gram, half, 1)
        turned = jnp.where(lane2 < half, -turned, turned)
        quad = jnp.concatenate([spread_rows(gram, diag_b), spread_rows(turned, diag_b)], axis=0)
        vec = jnp.concatenate([d_r, d_i], axis=0)
        energy = jnp.sum(vec * mm(quad.astype(BF), vec.astype(BF), ((1,), (0,))), axis=0, keepdims=True)
        factor = 1.0 / jnp.sqrt(energy / entries + 1e-06)
        fac = jnp.transpose(jnp.broadcast_to(factor, (pts, lanes)))
        s_g = sh[top : top + 2 * half]
        for c in range(2):
            d = jnp.concatenate([d_r, -d_i] if c == 0 else [d_i, d_r], axis=0)
            field = mm(jnp.transpose(d).astype(BF), s_g, ((1,), (0,)))
            for v in range(nvar):
                val = (field[:, v * pts : (v + 1) * pts] * fac).astype(BF).reshape(GROUP, modes, pts)
                ob[c, f0 : f0 + nf, v] = val[:nf]
        cp = pltpu.make_async_copy(ob.at[:, pl.ds(f0, nf)], new_out.at[:, pl.ds(f0, nf)], o_sem.at[g])
        cp.start()
        copies.append(cp)

    mode_row = lax.broadcasted_iota(jnp.int32, (blocks, modes, lanes), 1)
    pick = mode_row == lax.broadcasted_iota(jnp.int32, (blocks, modes, lanes), 2) % modes
    e_row = lax.broadcasted_iota(jnp.int32, (lanes, freqs), 0) // modes
    e_col = lax.broadcasted_iota(jnp.int32, (lanes, freqs), 1)
    moves = [jnp.where(e_col == e_row + g * GROUP, 1.0, 0.0).astype(BF) for g in range(groups)]
    move = jnp.concatenate(moves + moves, axis=0)
    for c in range(2):
        his, los = [], []
        for g in range(groups):
            val = held[g][c]
            if g == groups - 1:
                val = jnp.where(lane2 < (freqs - g * GROUP) * modes, val, 0.0)
            hi = val.astype(BF).astype(F32)
            for part, to in ((hi, his), (val - hi, los)):
                big = jnp.broadcast_to(part[:, None, :], (blocks, modes, lanes))
                to.append(jnp.where(pick, big, 0.0).reshape(blocks * modes, lanes).astype(BF))
        moved = mm(jnp.concatenate(his + los, axis=1), move, ((1,), (0,)))
        coef_out[c] = moved.reshape(blocks, modes, freqs)
    for cp in copies:
        cp.wait()


def solution(mesh):
    n_tm, n_sp = mesh.shape["tm"], mesh.shape["space"]
    n = n_tm * n_sp

    def on_device(snapshots, basis, mass_table, elem_kind, offsets):
        rows, nvar, slab = snapshots.shape
        _, freqs, modes, _, pts = basis.shape
        blocks = offsets.shape[0]
        groups = -(-freqs // GROUP)
        entries = nvar * pts * n
        units = 3 * groups
        low = math.gcd(n_tm, 4)
        side = low * n_sp
        upo = -(-units // side)
        owners = -(-units // upo)
        table_rows = groups * 2 * GROUP * blocks
        unit = (blocks, GROUP * modes)
        chunks = tuple((v, min(v + 2, nvar)) for v in range(0, nvar, 2))
        snap = jnp.transpose(snapshots, (1, 0, 2))
        base = jnp.transpose(basis, (0, 1, 3, 2, 4))
        hbm = pl.BlockSpec(memory_space=pltpu.HBM)
        vmem = pl.BlockSpec(memory_space=pltpu.VMEM)
        spec, total = pl.pallas_call(
            functools.partial(kernel, n_tm, n_sp, low, entries, chunks),
            out_shape=(
                jax.ShapeDtypeStruct((table_rows, nvar * pts), BF),
                jax.ShapeDtypeStruct((owners * upo,) + unit, F32),
            ),
            in_specs=[hbm] * 5,
            out_specs=(vmem, vmem),
            scratch_shapes=[
                pltpu.VMEM((table_rows, rows * n_tm), BF),
                pltpu.VMEM((2, groups * GROUP, nvar, modes, pts), BF),
                pltpu.VMEM((owners * upo,) + unit, F32),
                pltpu.VMEM((n_tm // low, upo) + unit, F32),
                pltpu.VMEM((side, upo) + unit, F32),
                pltpu.VMEM((owners * upo,) + unit, F32),
                pltpu.VMEM(mass_table.shape, F32),
                pltpu.SMEM(elem_kind.shape, jnp.int32),
                pltpu.SMEM(offsets.shape, jnp.int32),
            ]
            + [pltpu.VMEM((n_tm, v1 - v0, rows, pts), BF) for v0, v1 in chunks]
            + [
                pltpu.SemaphoreType.DMA((len(chunks),)),
                pltpu.SemaphoreType.DMA((len(chunks),)),
                pltpu.SemaphoreType.DMA((4,)),
            ]
            + [pltpu.SemaphoreType.DMA] * 6,
            compiler_params=pltpu.CompilerParams(
                collective_id=0, has_side_effects=True, vmem_limit_bytes=48 * 1024 * 1024
            ),
        )(*[pltpu.with_memory_space_constraint(a, pltpu.HBM) for a in (snap, base, mass_table, elem_kind, offsets)])
        coef, new = pl.pallas_call(
            functools.partial(finish, entries),
            out_shape=(
                jax.ShapeDtypeStruct((2, blocks, modes, freqs), F32),
                jax.ShapeDtypeStruct(base.shape, BF),
            ),
            in_specs=[vmem, vmem],
            out_specs=(vmem, hbm),
            scratch_shapes=[pltpu.VMEM(base.shape, BF), pltpu.SemaphoreType.DMA((groups,))],
            compiler_params=pltpu.CompilerParams(vmem_limit_bytes=32 * 1024 * 1024),
        )(total, spec)
        return jnp.transpose(coef, (0, 3, 1, 2)), jnp.transpose(new, (0, 1, 3, 2, 4))

    return jax.shard_map(
        on_device,
        mesh=mesh,
        in_specs=(
            P("tm", None, "space"),
            P(None, None, None, None, ("space", "tm")),
            P(),
            P(("space", "tm")),
            P(),
        ),
        out_specs=(P(), P(None, None, None, None, ("space", "tm"))),
        check_vma=False,
    )
```

```python
import functools
import math

import jax
import jax.numpy as jnp
from jax import lax
from jax.experimental import pallas as pl
from jax.experimental.pallas import tpu as pltpu
from jax.sharding import PartitionSpec as P

NT = 256
GROUP = 8
MESH = pl.DeviceIdType.MESH
BF = jnp.bfloat16
F32 = jnp.float32


def mm(a, b, contract):
    return lax.dot_general(a, b, (contract, ((), ())), preferred_element_type=F32)


def kernel(
    n_tm, n_sp, low, entries, chunks,
    snap, basis, mass_in, kinds_in, offs_in,
    sh, y_out,
    table, ub, xb, line, plane, yb, mass, kinds, offs, *rest,
):
    recs, (a_send, a_recv, l_sem, s1, r1, s2, r2, s3, r3) = rest[: len(chunks)], rest[len(chunks) :]
    tm = lax.axis_index("tm")
    sp = lax.axis_index("space")
    high = n_tm // low
    side = low * n_sp
    mid = n_tm // 2
    turn = lax.rem(tm + n_tm - n_tm // 4, n_tm)
    spot = lax.div(turn, mid) * (side // 2) + sp * mid + lax.rem(turn, mid)
    level = lax.div(tm, low)
    freqs = basis.shape[1]
    rows, pts = recs[0].shape[2:]
    groups = sh.shape[0] // (2 * GROUP * 8)
    record = n_tm * rows
    blocks = offs.shape[0]
    modes = basis.shape[3]
    upo = plane.shape[1]
    owners = xb.shape[0] // upo
    half = GROUP * blocks
    lanes = GROUP * modes

    def beside(p):
        r = lax.rem(p, side // 2)
        back = lax.div(p, side // 2) * mid + lax.rem(r, mid)
        return {"tm": lax.rem(back + n_tm // 4, n_tm), "space": lax.div(r, mid)}

    barrier = pltpu.get_barrier_semaphore()

    def greet_line(i, carry):
        pl.semaphore_signal(
            barrier, inc=1, device_id={"tm": lax.rem(tm + i, n_tm), "space": sp}, device_id_type=MESH
        )
        return carry

    def greet_side(i, carry):
        to = lax.rem(sp + lax.div(i, low), n_sp)
        pl.semaphore_signal(
            barrier, inc=1, device_id={"tm": level * low + lax.rem(i, low), "space": to}, device_id_type=MESH
        )
        return carry

    lax.fori_loop(1, n_tm, greet_line, 0)
    lax.fori_loop(low, side, greet_side, 0)
    loads = [
        pltpu.make_async_copy(offs_in, offs, l_sem.at[0]),
        pltpu.make_async_copy(kinds_in, kinds, l_sem.at[1]),
        pltpu.make_async_copy(mass_in, mass, l_sem.at[2]),
        pltpu.make_async_copy(basis, ub.at[:, pl.ds(0, freqs)], l_sem.at[3]),
    ]
    for cp in loads:
        cp.start()
    pl.semaphore_wait(barrier, n_tm - 1 + side - low)

    for ci, (v0, v1) in enumerate(chunks):

        def block(to):
            return snap.at[pl.ds(v0, v1 - v0), :, pl.ds(pl.multiple_of(to * pts, pts), pts)]

        def send(i, carry):
            d = lax.div(i + 1, 2)
            to = lax.rem(tm + n_tm // 2 + jnp.where(lax.rem(i, 2) == 0, d, -d) + n_tm, n_tm)
            pltpu.make_async_remote_copy(
                block(to), recs[ci].at[tm], a_send.at[ci], a_recv.at[ci],
                device_id={"tm": to, "space": sp}, device_id_type=MESH,
            ).start()
            return carry

        lax.fori_loop(0, n_tm - 1, send, 0)
        pltpu.make_async_copy(block(tm), recs[ci].at[tm], a_recv.at[ci]).start()

    loads[0].wait()
    row = lax.broadcasted_iota(jnp.int32, (blocks, record), 0)
    lag = lax.broadcasted_iota(jnp.int32, (blocks, record), 1)
    for b in range(blocks):
        lag = jnp.where(row == b, lag - offs[b], lag)
    inside = (lag >= 0) & (lag < NT)
    theta = jnp.clip(lag, 0, NT - 1).astype(F32) * (2.0 * math.pi / NT)
    c1, s1v = jnp.cos(theta), jnp.sin(theta)
    win = jnp.where(inside, (0.5 - 0.5 * c1) * (1.0 / math.sqrt(0.375 * NT)), 0.0)
    cc, ss = win, jnp.zeros_like(win)
    for f in range(0, groups * GROUP, 2):
        c_next, s_next = cc * c1 - ss * s1v, ss * c1 + cc * s1v
        at = (f // GROUP) * 2 * half + (f % GROUP) * blocks
        table[at : at + 2 * blocks] = jnp.concatenate([cc, c_next], axis=0).astype(BF)
        table[at + half : at + half + 2 * blocks] = jnp.concatenate([-ss, -s_next], axis=0).astype(BF)
        cc, ss = c_next * c1 - s_next * s1v, s_next * c1 + c_next * s1v

    loads[1].wait()
    loads[2].wait()
    size = mass.shape[1]
    elems = pts // size
    strips = []
    for e in range(elems):
        kind = jnp.full((size, size), kinds[e], jnp.int32)
        blk = mass[0]
        for k in range(1, mass.shape[0]):
            blk = jnp.where(kind == k, mass[k], blk)
        zero = jnp.zeros_like(blk)
        strips.append(jnp.concatenate([blk if j == e else zero for j in range(elems)], axis=1))
    m_all = jnp.concatenate(strips, axis=0)
    m_hi = m_all.astype(BF)
    m_lo = (m_all - m_hi.astype(F32)).astype(BF)
    m_stack = jnp.concatenate([m_hi, m_hi, m_lo], axis=0)

    loads[3].wait()
    ub[:, freqs:] = jnp.zeros((2, groups * GROUP - freqs) + ub.shape[2:], BF)

    row_f = lax.broadcasted_iota(jnp.int32, (GROUP, blocks, lanes), 0)
    lane = lax.broadcasted_iota(jnp.int32, (GROUP, blocks, lanes), 2)
    diag_k = row_f == lane // modes
    diag_b = row_f == (lane % half) // blocks
    lane2 = lax.broadcasted_iota(jnp.int32, (blocks, lanes), 1)

    def fold(full, mask):
        return jnp.sum(jnp.where(mask, full.reshape(GROUP, blocks, lanes), 0.0), axis=0)

    total = [None] * (3 * groups)
    for ci, (v0, v1) in enumerate(chunks):
        rec = recs[ci]
        pltpu.make_async_copy(rec, rec, a_recv.at[ci]).wait()
        count = v1 - v0
        x = jnp.concatenate([rec[:, v].reshape(record, pts) for v in range(count)], axis=1)
        spec = mm(table[...], x, ((1,), (0,)))
        s_hi = spec.astype(BF)
        s_lo = (spec - s_hi.astype(F32)).astype(BF)
        sh[:, v0 * pts : v1 * pts] = s_hi
        wts = []
        for v in range(count):
            cut = slice(v * pts, (v + 1) * pts)
            lhs = jnp.concatenate([s_hi[:, cut], s_lo[:, cut], s_hi[:, cut]], axis=1)
            wts.append(mm(lhs, m_stack, ((1,), (0,))).astype(BF))
        wt = jnp.concatenate(wts, axis=1)
        for g in range(groups):
            top = g * 2 * half
            f0 = g * GROUP
            u = [
                jnp.concatenate(
                    [ub[c, f0 : f0 + GROUP, v].reshape(lanes, pts) for v in range(v0, v1)], axis=1
                )
                for c in range(2)
            ]
            lhs = jnp.concatenate(u + [s_hi[top : top + 2 * half]], axis=0)
            full = mm(wt[top : top + 2 * half], lhs, ((1,), (1,)))
            rr = fold(full[:half, :lanes], diag_k)
            ri = fold(full[:half, lanes : 2 * lanes], diag_k)
            ir = fold(full[half:, :lanes], diag_k)
            ii = fold(full[half:, lanes : 2 * lanes], diag_k)
            p_r = fold(full[:half, 2 * lanes :], diag_b)
            p_i = pltpu.roll(fold(full[half:, 2 * lanes :], diag_b), half, 1)
            new = [rr + ii, ir - ri, jnp.where(lane2 < half, p_r + p_i, p_i - p_r)]
            for j in range(3):
                at = 3 * g + j
                total[at] = new[j] if ci == 0 else total[at] + new[j]
    for at in range(3 * groups):
        xb[at] = total[at]

    mine = pl.ds(spot * upo, upo)

    def scatter(i, carry):
        o = lax.rem(spot + i, owners)

        @pl.when(o != spot)
        def _():
            pltpu.make_async_remote_copy(
                xb.at[pl.ds(o * upo, upo)], plane.at[spot], s1, r1,
                device_id=beside(o), device_id_type=MESH,
            ).start()

        return carry

    lax.fori_loop(0, owners, scatter, 0)

    def wait_bytes(ref, sem):
        pltpu.make_async_copy(ref, ref, sem).wait()

    @pl.when(spot < owners)
    def _():
        plane[spot] = xb[mine]
        wait_bytes(plane.at[pl.ds(0, side - 1)], r1)
        line[level] = jnp.sum(plane[...], axis=0)

        def exchange(i, carry):
            to = lax.rem(level + i, high) * low + lax.rem(tm, low)
            pltpu.make_async_remote_copy(
                line.at[level], line.at[level], s2, r2,
                device_id={"tm": to, "space": sp}, device_id_type=MESH,
            ).start()
            return carry

        if high > 1:
            lax.fori_loop(1, high, exchange, 0)
            wait_bytes(line.at[pl.ds(0, high - 1)], r2)
        yb[mine] = jnp.sum(line[...], axis=0)

        def gather(i, carry):
            pltpu.make_async_remote_copy(
                yb.at[mine], yb.at[mine], s3, r3,
                device_id=beside(lax.rem(spot + i, side)), device_id_type=MESH,
            ).start()
            return carry

        lax.fori_loop(1, side, gather, 0)
        wait_bytes(yb.at[pl.ds(0, (owners - 1) * upo)], r3)

    @pl.when(spot >= owners)
    def _():
        wait_bytes(yb, r3)

    y_out[...] = yb[...]
    for ci in range(len(chunks)):
        wait_bytes(recs[ci].at[pl.ds(0, n_tm - 1)], a_send.at[ci])

    @pl.when(spot < owners)
    def _():
        wait_bytes(xb.at[pl.ds(0, (owners - 1) * upo)], s1)
        if high > 1:
            wait_bytes(line.at[pl.ds(0, high - 1)], s2)
        wait_bytes(plane.at[pl.ds(0, side - 1)], s3)

    @pl.when(spot >= owners)
    def _():
        wait_bytes(xb, s1)


def finish(entries, yb, sh, coef_out, new_out, ob, o_sem):
    freqs, nvar, modes, pts = new_out.shape[1:]
    blocks = coef_out.shape[1]
    half = GROUP * blocks
    lanes = GROUP * modes
    groups = -(-freqs // GROUP)
    row_f = lax.broadcasted_iota(jnp.int32, (GROUP, blocks, lanes), 0)
    lane = lax.broadcasted_iota(jnp.int32, (GROUP, blocks, lanes), 2)
    diag_k = row_f == lane // modes
    diag_b = row_f == (lane % half) // blocks
    lane2 = lax.broadcasted_iota(jnp.int32, (blocks, lanes), 1)
    scale = 1.0 / math.sqrt(entries)

    def spread_rows(val, mask):
        big = jnp.broadcast_to(val[None], (GROUP, blocks, lanes))
        return jnp.where(mask, big, 0.0).reshape(half, lanes)

    copies, held = [], []
    for g in range(groups):
        top = g * 2 * half
        f0 = g * GROUP
        nf = min(GROUP, freqs - f0)
        co = [yb[3 * g + c] * scale for c in range(2)]
        held.append(co)
        cr, ci = [v.astype(BF).astype(F32) for v in co]
        gram = yb[3 * g + 2]
        d_r, d_i = spread_rows(cr, diag_k), spread_rows(ci, diag_k)
        turned = pltpu.roll(gram, half, 1)
        turned = jnp.where(lane2 < half, -turned, turned)
        quad = jnp.concatenate([spread_rows(gram, diag_b), spread_rows(turned, diag_b)], axis=0)
        vec = jnp.concatenate([d_r, d_i], axis=0)
        energy = jnp.sum(vec * mm(quad.astype(BF), vec.astype(BF), ((1,), (0,))), axis=0, keepdims=True)
        factor = 1.0 / jnp.sqrt(energy / entries + 1e-06)
        fac = jnp.transpose(jnp.broadcast_to(factor, (pts, lanes)))
        s_g = sh[top : top + 2 * half]
        for c in range(2):
            d = jnp.concatenate([d_r, -d_i] if c == 0 else [d_i, d_r], axis=0)
            field = mm(jnp.transpose(d).astype(BF), s_g, ((1,), (0,)))
            for v in range(nvar):
                val = (field[:, v * pts : (v + 1) * pts] * fac).astype(BF).reshape(GROUP, modes, pts)
                ob[c, f0 : f0 + nf, v] = val[:nf]
        cp = pltpu.make_async_copy(ob.at[:, pl.ds(f0, nf)], new_out.at[:, pl.ds(f0, nf)], o_sem.at[g])
        cp.start()
        copies.append(cp)

    mode_row = lax.broadcasted_iota(jnp.int32, (blocks, modes, lanes), 1)
    pick = mode_row == lax.broadcasted_iota(jnp.int32, (blocks, modes, lanes), 2) % modes
    e_row = lax.broadcasted_iota(jnp.int32, (lanes, freqs), 0) // modes
    e_col = lax.broadcasted_iota(jnp.int32, (lanes, freqs), 1)
    moves = [jnp.where(e_col == e_row + g * GROUP, 1.0, 0.0).astype(BF) for g in range(groups)]
    move = jnp.concatenate(moves + moves, axis=0)
    for c in range(2):
        his, los = [], []
        for g in range(groups):
            val = held[g][c]
            if g == groups - 1:
                val = jnp.where(lane2 < (freqs - g * GROUP) * modes, val, 0.0)
            hi = val.astype(BF).astype(F32)
            for part, to in ((hi, his), (val - hi, los)):
                big = jnp.broadcast_to(part[:, None, :], (blocks, modes, lanes))
                to.append(jnp.where(pick, big, 0.0).reshape(blocks * modes, lanes).astype(BF))
        moved = mm(jnp.concatenate(his + los, axis=1), move, ((1,), (0,)))
        coef_out[c] = moved.reshape(blocks, modes, freqs)
    for cp in copies:
        cp.wait()


def solution(mesh):
    n_tm, n_sp = mesh.shape["tm"], mesh.shape["space"]
    n = n_tm * n_sp

    def on_device(snapshots, basis, mass_table, elem_kind, offsets):
        rows, nvar, slab = snapshots.shape
        _, freqs, modes, _, pts = basis.shape
        blocks = offsets.shape[0]
        groups = -(-freqs // GROUP)
        entries = nvar * pts * n
        units = 3 * groups
        low = n_tm
        side = low * n_sp
        upo = -(-units // side)
        owners = -(-units // upo)
        table_rows = groups * 2 * GROUP * blocks
        unit = (blocks, GROUP * modes)
        chunks = tuple((v, min(v + 2, nvar)) for v in range(0, nvar, 2))
        snap = jnp.transpose(snapshots, (1, 0, 2))
        base = jnp.transpose(basis, (0, 1, 3, 2, 4))
        hbm = pl.BlockSpec(memory_space=pltpu.HBM)
        vmem = pl.BlockSpec(memory_space=pltpu.VMEM)
        spec, total = pl.pallas_call(
            functools.partial(kernel, n_tm, n_sp, low, entries, chunks),
            out_shape=(
                jax.ShapeDtypeStruct((table_rows, nvar * pts), BF),
                jax.ShapeDtypeStruct((owners * upo,) + unit, F32),
            ),
            in_specs=[hbm] * 5,
            out_specs=(vmem, vmem),
            scratch_shapes=[
                pltpu.VMEM((table_rows, rows * n_tm), BF),
                pltpu.VMEM((2, groups * GROUP, nvar, modes, pts), BF),
                pltpu.VMEM((owners * upo,) + unit, F32),
                pltpu.VMEM((n_tm // low, upo) + unit, F32),
                pltpu.VMEM((side, upo) + unit, F32),
                pltpu.VMEM((owners * upo,) + unit, F32),
                pltpu.VMEM(mass_table.shape, F32),
                pltpu.SMEM(elem_kind.shape, jnp.int32),
                pltpu.SMEM(offsets.shape, jnp.int32),
            ]
            + [pltpu.VMEM((n_tm, v1 - v0, rows, pts), BF) for v0, v1 in chunks]
            + [
                pltpu.SemaphoreType.DMA((len(chunks),)),
                pltpu.SemaphoreType.DMA((len(chunks),)),
                pltpu.SemaphoreType.DMA((4,)),
            ]
            + [pltpu.SemaphoreType.DMA] * 6,
            compiler_params=pltpu.CompilerParams(
                collective_id=0, has_side_effects=True, vmem_limit_bytes=48 * 1024 * 1024
            ),
        )(*[pltpu.with_memory_space_constraint(a, pltpu.HBM) for a in (snap, base, mass_table, elem_kind, offsets)])
        coef, new = pl.pallas_call(
            functools.partial(finish, entries),
            out_shape=(
                jax.ShapeDtypeStruct((2, blocks, modes, freqs), F32),
                jax.ShapeDtypeStruct(base.shape, BF),
            ),
            in_specs=[vmem, vmem],
            out_specs=(vmem, hbm),
            scratch_shapes=[pltpu.VMEM(base.shape, BF), pltpu.SemaphoreType.DMA((groups,))],
            compiler_params=pltpu.CompilerParams(vmem_limit_bytes=32 * 1024 * 1024),
        )(total, spec)
        return jnp.transpose(coef, (0, 3, 1, 2)), jnp.transpose(new, (0, 1, 3, 2, 4))

    return jax.shard_map(
        on_device,
        mesh=mesh,
        in_specs=(
            P("tm", None, "space"),
            P(None, None, None, None, ("space", "tm")),
            P(),
            P(("space", "tm")),
            P(),
        ),
        out_specs=(P(), P(None, None, None, None, ("space", "tm"))),
        check_vma=False,
    )
```

```python
import functools
import math

import jax
import jax.numpy as jnp
from jax import lax
from jax.experimental import pallas as pl
from jax.experimental.pallas import tpu as pltpu
from jax.sharding import PartitionSpec as P

NT = 256
GROUP = 8
MESH = pl.DeviceIdType.MESH
BF = jnp.bfloat16
F32 = jnp.float32


def mm(a, b, contract):
    return lax.dot_general(a, b, (contract, ((), ())), preferred_element_type=F32)


def kernel(
    n_tm, n_sp, low, entries, chunks,
    snap, basis, mass_in, kinds_in, offs_in,
    sh, y_out,
    table, ub, xb, line, plane, yb, mass, kinds, offs, *rest,
):
    recs, (a_send, a_recv, l_sem, s1, r1, s2, r2, s3, r3) = rest[: len(chunks)], rest[len(chunks) :]
    tm = lax.axis_index("tm")
    sp = lax.axis_index("space")
    high = n_tm // low
    side = low * n_sp
    mid = n_tm // 2
    turn = lax.rem(tm + n_tm - n_tm // 4, n_tm)
    spot = lax.div(turn, mid) * (side // 2) + sp * mid + lax.rem(turn, mid)
    level = lax.div(tm, low)
    freqs = basis.shape[1]
    rows, pts = recs[0].shape[2:]
    groups = sh.shape[0] // (2 * GROUP * 8)
    record = n_tm * rows
    blocks = offs.shape[0]
    modes = basis.shape[3]
    upo = plane.shape[1]
    owners = xb.shape[0] // upo
    half = GROUP * blocks
    lanes = GROUP * modes

    def beside(p):
        r = lax.rem(p, side // 2)
        back = lax.div(p, side // 2) * mid + lax.rem(r, mid)
        return {"tm": lax.rem(back + n_tm // 4, n_tm), "space": lax.div(r, mid)}

    barrier = pltpu.get_barrier_semaphore()

    def greet_line(i, carry):
        pl.semaphore_signal(
            barrier, inc=1, device_id={"tm": lax.rem(tm + i, n_tm), "space": sp}, device_id_type=MESH
        )
        return carry

    def greet_side(i, carry):
        to = lax.rem(sp + lax.div(i, low), n_sp)
        pl.semaphore_signal(
            barrier, inc=1, device_id={"tm": level * low + lax.rem(i, low), "space": to}, device_id_type=MESH
        )
        return carry

    lax.fori_loop(1, n_tm, greet_line, 0, unroll=side <= 32)
    lax.fori_loop(low, side, greet_side, 0, unroll=side <= 32)
    loads = [
        pltpu.make_async_copy(offs_in, offs, l_sem.at[0]),
        pltpu.make_async_copy(kinds_in, kinds, l_sem.at[1]),
        pltpu.make_async_copy(mass_in, mass, l_sem.at[2]),
        pltpu.make_async_copy(basis, ub.at[:, pl.ds(0, freqs)], l_sem.at[3]),
    ]
    for cp in loads:
        cp.start()
    pl.semaphore_wait(barrier, n_tm - 1 + side - low)

    for ci, (v0, v1) in enumerate(chunks):

        def block(to):
            return snap.at[pl.ds(v0, v1 - v0), :, pl.ds(pl.multiple_of(to * pts, pts), pts)]

        def send(i, carry):
            d = lax.div(i + 1, 2)
            to = lax.rem(tm + n_tm // 2 + jnp.where(lax.rem(i, 2) == 0, d, -d) + n_tm, n_tm)
            pltpu.make_async_remote_copy(
                block(to), recs[ci].at[tm], a_send.at[ci], a_recv.at[ci],
                device_id={"tm": to, "space": sp}, device_id_type=MESH,
            ).start()
            return carry

        lax.fori_loop(0, n_tm - 1, send, 0, unroll=side <= 32)
        pltpu.make_async_copy(block(tm), recs[ci].at[tm], a_recv.at[ci]).start()

    loads[0].wait()
    row = lax.broadcasted_iota(jnp.int32, (blocks, record), 0)
    lag = lax.broadcasted_iota(jnp.int32, (blocks, record), 1)
    for b in range(blocks):
        lag = jnp.where(row == b, lag - offs[b], lag)
    inside = (lag >= 0) & (lag < NT)
    theta = jnp.clip(lag, 0, NT - 1).astype(F32) * (2.0 * math.pi / NT)
    c1, s1v = jnp.cos(theta), jnp.sin(theta)
    win = jnp.where(inside, (0.5 - 0.5 * c1) * (1.0 / math.sqrt(0.375 * NT)), 0.0)
    cc, ss = win, jnp.zeros_like(win)
    for f in range(0, groups * GROUP, 2):
        c_next, s_next = cc * c1 - ss * s1v, ss * c1 + cc * s1v
        at = (f // GROUP) * 2 * half + (f % GROUP) * blocks
        table[at : at + 2 * blocks] = jnp.concatenate([cc, c_next], axis=0).astype(BF)
        table[at + half : at + half + 2 * blocks] = jnp.concatenate([-ss, -s_next], axis=0).astype(BF)
        cc, ss = c_next * c1 - s_next * s1v, s_next * c1 + c_next * s1v

    loads[1].wait()
    loads[2].wait()
    size = mass.shape[1]
    elems = pts // size
    strips = []
    for e in range(elems):
        kind = jnp.full((size, size), kinds[e], jnp.int32)
        blk = mass[0]
        for k in range(1, mass.shape[0]):
            blk = jnp.where(kind == k, mass[k], blk)
        zero = jnp.zeros_like(blk)
        strips.append(jnp.concatenate([blk if j == e else zero for j in range(elems)], axis=1))
    m_all = jnp.concatenate(strips, axis=0)
    m_hi = m_all.astype(BF)
    m_lo = (m_all - m_hi.astype(F32)).astype(BF)
    m_stack = jnp.concatenate([m_hi, m_hi, m_lo], axis=0)

    loads[3].wait()
    ub[:, freqs:] = jnp.zeros((2, groups * GROUP - freqs) + ub.shape[2:], BF)

    row_f = lax.broadcasted_iota(jnp.int32, (GROUP, blocks, lanes), 0)
    lane = lax.broadcasted_iota(jnp.int32, (GROUP, blocks, lanes), 2)
    diag_k = row_f == lane // modes
    diag_b = row_f == (lane % half) // blocks
    lane2 = lax.broadcasted_iota(jnp.int32, (blocks, lanes), 1)

    def fold(full, mask):
        return jnp.sum(jnp.where(mask, full.reshape(GROUP, blocks, lanes), 0.0), axis=0)

    total = [None] * (3 * groups)
    for ci, (v0, v1) in enumerate(chunks):
        rec = recs[ci]
        pltpu.make_async_copy(rec, rec, a_recv.at[ci]).wait()
        count = v1 - v0
        x = jnp.concatenate([rec[:, v].reshape(record, pts) for v in range(count)], axis=1)
        spec = mm(table[...], x, ((1,), (0,)))
        s_hi = spec.astype(BF)
        s_lo = (spec - s_hi.astype(F32)).astype(BF)
        sh[:, v0 * pts : v1 * pts] = s_hi
        wts = []
        for v in range(count):
            cut = slice(v * pts, (v + 1) * pts)
            lhs = jnp.concatenate([s_hi[:, cut], s_lo[:, cut], s_hi[:, cut]], axis=1)
            wts.append(mm(lhs, m_stack, ((1,), (0,))).astype(BF))
        wt = jnp.concatenate(wts, axis=1)
        for g in range(groups):
            top = g * 2 * half
            f0 = g * GROUP
            u = [
                jnp.concatenate(
                    [ub[c, f0 : f0 + GROUP, v].reshape(lanes, pts) for v in range(v0, v1)], axis=1
                )
                for c in range(2)
            ]
            lhs = jnp.concatenate(u + [s_hi[top : top + 2 * half]], axis=0)
            full = mm(wt[top : top + 2 * half], lhs, ((1,), (1,)))
            rr = fold(full[:half, :lanes], diag_k)
            ri = fold(full[:half, lanes : 2 * lanes], diag_k)
            ir = fold(full[half:, :lanes], diag_k)
            ii = fold(full[half:, lanes : 2 * lanes], diag_k)
            p_r = fold(full[:half, 2 * lanes :], diag_b)
            p_i = pltpu.roll(fold(full[half:, 2 * lanes :], diag_b), half, 1)
            new = [rr + ii, ir - ri, jnp.where(lane2 < half, p_r + p_i, p_i - p_r)]
            for j in range(3):
                at = 3 * g + j
                total[at] = new[j] if ci == 0 else total[at] + new[j]
    for at in range(3 * groups):
        xb[at] = total[at]

    mine = pl.ds(spot * upo, upo)

    def scatter(i, carry):
        o = lax.rem(spot + i, owners)

        @pl.when(o != spot)
        def _():
            pltpu.make_async_remote_copy(
                xb.at[pl.ds(o * upo, upo)], plane.at[spot], s1, r1,
                device_id=beside(o), device_id_type=MESH,
            ).start()

        return carry

    lax.fori_loop(0, owners, scatter, 0, unroll=side <= 32)

    def wait_bytes(ref, sem):
        pltpu.make_async_copy(ref, ref, sem).wait()

    @pl.when(spot < owners)
    def _():
        plane[spot] = xb[mine]
        wait_bytes(plane.at[pl.ds(0, side - 1)], r1)
        line[level] = jnp.sum(plane[...], axis=0)

        def exchange(i, carry):
            to = lax.rem(level + i, high) * low + lax.rem(tm, low)
            pltpu.make_async_remote_copy(
                line.at[level], line.at[level], s2, r2,
                device_id={"tm": to, "space": sp}, device_id_type=MESH,
            ).start()
            return carry

        if high > 1:
            lax.fori_loop(1, high, exchange, 0)
            wait_bytes(line.at[pl.ds(0, high - 1)], r2)
        yb[mine] = jnp.sum(line[...], axis=0)

        def gather(i, carry):
            pltpu.make_async_remote_copy(
                yb.at[mine], yb.at[mine], s3, r3,
                device_id=beside(lax.rem(spot + i, side)), device_id_type=MESH,
            ).start()
            return carry

        lax.fori_loop(1, side, gather, 0, unroll=side <= 32)
        wait_bytes(yb.at[pl.ds(0, (owners - 1) * upo)], r3)

    @pl.when(spot >= owners)
    def _():
        wait_bytes(yb, r3)

    y_out[...] = yb[...]
    for ci in range(len(chunks)):
        wait_bytes(recs[ci].at[pl.ds(0, n_tm - 1)], a_send.at[ci])

    @pl.when(spot < owners)
    def _():
        wait_bytes(xb.at[pl.ds(0, (owners - 1) * upo)], s1)
        if high > 1:
            wait_bytes(line.at[pl.ds(0, high - 1)], s2)
        wait_bytes(plane.at[pl.ds(0, side - 1)], s3)

    @pl.when(spot >= owners)
    def _():
        wait_bytes(xb, s1)


def finish(entries, yb, sh, coef_out, new_out, ob, o_sem):
    freqs, nvar, modes, pts = new_out.shape[1:]
    blocks = coef_out.shape[1]
    half = GROUP * blocks
    lanes = GROUP * modes
    groups = -(-freqs // GROUP)
    row_f = lax.broadcasted_iota(jnp.int32, (GROUP, blocks, lanes), 0)
    lane = lax.broadcasted_iota(jnp.int32, (GROUP, blocks, lanes), 2)
    diag_k = row_f == lane // modes
    diag_b = row_f == (lane % half) // blocks
    lane2 = lax.broadcasted_iota(jnp.int32, (blocks, lanes), 1)
    scale = 1.0 / math.sqrt(entries)

    def spread_rows(val, mask):
        big = jnp.broadcast_to(val[None], (GROUP, blocks, lanes))
        return jnp.where(mask, big, 0.0).reshape(half, lanes)

    copies, held = [], []
    for g in range(groups):
        top = g * 2 * half
        f0 = g * GROUP
        nf = min(GROUP, freqs - f0)
        co = [yb[3 * g + c] * scale for c in range(2)]
        held.append(co)
        cr, ci = [v.astype(BF).astype(F32) for v in co]
        gram = yb[3 * g + 2]
        d_r, d_i = spread_rows(cr, diag_k), spread_rows(ci, diag_k)
        turned = pltpu.roll(gram, half, 1)
        turned = jnp.where(lane2 < half, -turned, turned)
        quad = jnp.concatenate([spread_rows(gram, diag_b), spread_rows(turned, diag_b)], axis=0)
        vec = jnp.concatenate([d_r, d_i], axis=0)
        energy = jnp.sum(vec * mm(quad.astype(BF), vec.astype(BF), ((1,), (0,))), axis=0, keepdims=True)
        factor = 1.0 / jnp.sqrt(energy / entries + 1e-06)
        fac = jnp.transpose(jnp.broadcast_to(factor, (pts, lanes)))
        s_g = sh[top : top + 2 * half]
        for c in range(2):
            d = jnp.concatenate([d_r, -d_i] if c == 0 else [d_i, d_r], axis=0)
            field = mm(jnp.transpose(d).astype(BF), s_g, ((1,), (0,)))
            for v in range(nvar):
                val = (field[:, v * pts : (v + 1) * pts] * fac).astype(BF).reshape(GROUP, modes, pts)
                ob[c, f0 : f0 + nf, v] = val[:nf]
        cp = pltpu.make_async_copy(ob.at[:, pl.ds(f0, nf)], new_out.at[:, pl.ds(f0, nf)], o_sem.at[g])
        cp.start()
        copies.append(cp)

    mode_row = lax.broadcasted_iota(jnp.int32, (blocks, modes, lanes), 1)
    pick = mode_row == lax.broadcasted_iota(jnp.int32, (blocks, modes, lanes), 2) % modes
    e_row = lax.broadcasted_iota(jnp.int32, (lanes, freqs), 0) // modes
    e_col = lax.broadcasted_iota(jnp.int32, (lanes, freqs), 1)
    moves = [jnp.where(e_col == e_row + g * GROUP, 1.0, 0.0).astype(BF) for g in range(groups)]
    move = jnp.concatenate(moves + moves, axis=0)
    for c in range(2):
        his, los = [], []
        for g in range(groups):
            val = held[g][c]
            if g == groups - 1:
                val = jnp.where(lane2 < (freqs - g * GROUP) * modes, val, 0.0)
            hi = val.astype(BF).astype(F32)
            for part, to in ((hi, his), (val - hi, los)):
                big = jnp.broadcast_to(part[:, None, :], (blocks, modes, lanes))
                to.append(jnp.where(pick, big, 0.0).reshape(blocks * modes, lanes).astype(BF))
        moved = mm(jnp.concatenate(his + los, axis=1), move, ((1,), (0,)))
        coef_out[c] = moved.reshape(blocks, modes, freqs)
    for cp in copies:
        cp.wait()


def solution(mesh):
    n_tm, n_sp = mesh.shape["tm"], mesh.shape["space"]
    n = n_tm * n_sp

    def on_device(snapshots, basis, mass_table, elem_kind, offsets):
        rows, nvar, slab = snapshots.shape
        _, freqs, modes, _, pts = basis.shape
        blocks = offsets.shape[0]
        groups = -(-freqs // GROUP)
        entries = nvar * pts * n
        units = 3 * groups
        low = n_tm
        side = low * n_sp
        upo = -(-units // side)
        owners = -(-units // upo)
        table_rows = groups * 2 * GROUP * blocks
        unit = (blocks, GROUP * modes)
        chunks = tuple((v, min(v + 2, nvar)) for v in range(0, nvar, 2))
        snap = jnp.transpose(snapshots, (1, 0, 2))
        base = jnp.transpose(basis, (0, 1, 3, 2, 4))
        hbm = pl.BlockSpec(memory_space=pltpu.HBM)
        vmem = pl.BlockSpec(memory_space=pltpu.VMEM)
        spec, total = pl.pallas_call(
            functools.partial(kernel, n_tm, n_sp, low, entries, chunks),
            out_shape=(
                jax.ShapeDtypeStruct((table_rows, nvar * pts), BF),
                jax.ShapeDtypeStruct((owners * upo,) + unit, F32),
            ),
            in_specs=[hbm] * 5,
            out_specs=(vmem, vmem),
            scratch_shapes=[
                pltpu.VMEM((table_rows, rows * n_tm), BF),
                pltpu.VMEM((2, groups * GROUP, nvar, modes, pts), BF),
                pltpu.VMEM((owners * upo,) + unit, F32),
                pltpu.VMEM((n_tm // low, upo) + unit, F32),
                pltpu.VMEM((side, upo) + unit, F32),
                pltpu.VMEM((owners * upo,) + unit, F32),
                pltpu.VMEM(mass_table.shape, F32),
                pltpu.SMEM(elem_kind.shape, jnp.int32),
                pltpu.SMEM(offsets.shape, jnp.int32),
            ]
            + [pltpu.VMEM((n_tm, v1 - v0, rows, pts), BF) for v0, v1 in chunks]
            + [
                pltpu.SemaphoreType.DMA((len(chunks),)),
                pltpu.SemaphoreType.DMA((len(chunks),)),
                pltpu.SemaphoreType.DMA((4,)),
            ]
            + [pltpu.SemaphoreType.DMA] * 6,
            compiler_params=pltpu.CompilerParams(
                collective_id=0, has_side_effects=True, vmem_limit_bytes=48 * 1024 * 1024
            ),
        )(*[pltpu.with_memory_space_constraint(a, pltpu.HBM) for a in (snap, base, mass_table, elem_kind, offsets)])
        coef, new = pl.pallas_call(
            functools.partial(finish, entries),
            out_shape=(
                jax.ShapeDtypeStruct((2, blocks, modes, freqs), F32),
                jax.ShapeDtypeStruct(base.shape, BF),
            ),
            in_specs=[vmem, vmem],
            out_specs=(vmem, hbm),
            scratch_shapes=[pltpu.VMEM(base.shape, BF), pltpu.SemaphoreType.DMA((groups,))],
            compiler_params=pltpu.CompilerParams(vmem_limit_bytes=32 * 1024 * 1024),
        )(total, spec)
        return jnp.transpose(coef, (0, 3, 1, 2)), jnp.transpose(new, (0, 1, 3, 2, 4))

    return jax.shard_map(
        on_device,
        mesh=mesh,
        in_specs=(
            P("tm", None, "space"),
            P(None, None, None, None, ("space", "tm")),
            P(),
            P(("space", "tm")),
            P(),
        ),
        out_specs=(P(), P(None, None, None, None, ("space", "tm"))),
        check_vma=False,
    )
```
